512 devices in a mesh: row: 16 (over x, y), col: 32 (over z, core).
Axes of the slice: x: 4, y: 4, z: 16, core: 2. Of those that a mesh axis runs over, the one named last changes fastest.
Arguments:
- rhs: float32 [6144, 12288], P('row', 'col'), may hold values from -6 to 6
- a_pair: float32 [6144, 24576], P('row', 'col'), may hold values from -0.15625 to 0.15625
- b_pair: float32 [12288, 12288], P('row', 'col'), may hold values from -0.15625 to 0.15625
- u_cay: float32 [6144, 384], P('row'), may hold values from -1 to 1, as said below
- v_cay: float32 [384, 12288], P(None, 'col'), may hold values from -1 to 1, as said below
Outputs:
- solved: float32 [6144, 12288], P('row', 'col')
The draws below stay inside these ranges and needn't reach their ends.
Inputs may be any that keep to these rules, and one draw needn't show every extreme that they name: `u_cay`: each 384 x 384 block of rows has spectral radius below 1. `v_cay`: each 384 x 384 block of columns has spectral radius below 1.
All inputs are finite; a program needn't handle non-finite values.
Results may differ from the reference program's by a relative error of at most 0.0001.
Values sent between devices are 32-bit elements; how exact they have to be, the bound alone decides.
No kernel may reach another device: no remote copies, remote signals or barrier semaphores. Data moves between devices by JAX's collectives and lax.ppermute only.
A program may use at most 64 MiB of HBM per device.

```python
import math
import jax
import jax.numpy as jnp
from jax import lax

NB = 384
ITERS = 3
N = 6144
M = 12288
FRONT = 15


def cayley_blocks(key, block_count):
    key_noise, key_size, key_signs = jax.random.split(key, 3)
    normal_draw = jax.random.normal(key_noise, (block_count, NB, NB), jnp.float32)
    symmetric = (normal_draw + jnp.swapaxes(normal_draw, 1, 2)) * (0.1 / math.sqrt(2.0 * NB))
    magnitude = jnp.exp(jax.random.uniform(key_size, (block_count, NB), jnp.float32, math.log(0.05), math.log(0.75)))
    signs = jnp.where(jax.random.bernoulli(key_signs, 0.5, (block_count, NB)), 1.0, -1.0)
    diagonal = jnp.eye(NB, dtype=jnp.float32)[None, :, :] * (signs * magnitude)[:, :, None]
    return symmetric + diagonal


def draw_u_cay(key, part):
    return cayley_blocks(jax.random.fold_in(key, 11), N // NB).reshape(N, NB)


def draw_v_cay(key, part):
    stacked = cayley_blocks(jax.random.fold_in(key, 12), M // NB)
    return stacked.transpose(1, 0, 2).reshape(NB, M)


def block_scale(key, dims, cuts, low, high):
    def one(position, parts):
        heights = jax.random.uniform(jax.random.fold_in(jax.random.fold_in(key, 6), position), (parts,), jnp.float32, low / len(cuts), high / len(cuts))
        return jnp.repeat(jnp.exp(heights), dims[position] // parts).reshape((-1,) + (1,) * (len(dims) - position - 1))

    loudness = one(*cuts[0])
    for cut in cuts[1:]:
        loudness = loudness * one(*cut)
    return loudness


def bell_draw(rng, extent, spread, most, shards=(), kind=jnp.bfloat16):
    values = spread * jax.random.normal(rng, extent, jnp.float32)
    if shards:
        values = values * block_scale(rng, extent, shards, -0.22, 0.18)
    return jnp.clip(values, -most, most).astype(kind)


def setup_inputs(seed: int = 0) -> dict:
    splits = jax.random.split(jax.random.key(seed), 6)
    rhs = bell_draw(splits[0], (N, M), 1.0, 6.0, ((0, 16), (1, 32)), jnp.float32)
    a_pair = bell_draw(splits[1], (N, 2 * M), (4 * NB) ** -0.5, 0.15625, ((0, 16), (1, 32)), jnp.float32)
    b_pair = bell_draw(splits[2], (2 * N, M), (4 * NB) ** -0.5, 0.15625, ((0, 16), (1, 32)), jnp.float32)
    u_cay = draw_u_cay(jax.random.fold_in(splits[5], 71), 0)
    v_cay = draw_v_cay(jax.random.fold_in(splits[5], 71), 0)
    return {"rhs": rhs, "a_pair": a_pair, "b_pair": b_pair, "u_cay": u_cay, "v_cay": v_cay}


precise = lax.Precision.HIGHEST


def product(left_side, right_side):
    return jnp.dot(left_side, right_side, precision=precise, preferred_element_type=jnp.float32)


def powers(matrix):
    result = [matrix]
    for step_index in range(ITERS - 1):
        result.append(product(result[-1], result[-1]))
    return result


def doubling(u_powers, v_powers, right_side):
    scaled = right_side + product(u_powers[0], right_side)
    iterate = 0.5 * (scaled + product(scaled, v_powers[0]))
    for u_power, v_power in zip(u_powers, v_powers):
        iterate = iterate + product(u_power, product(iterate, v_power))
    return iterate


def solve_block(u_block, v_block, right_side):
    return doubling(powers(u_block), powers(v_block), right_side)


def reference(rhs, a_pair, b_pair, u_cay, v_cay):
    row_count = N // NB
    col_count = M // NB
    blocks = rhs.reshape(row_count, NB, col_count, NB).transpose(0, 2, 1, 3)
    a_blocks = a_pair.reshape(row_count, NB, col_count, 2, NB).transpose(0, 2, 3, 1, 4)
    b_blocks = b_pair.reshape(row_count, 2, NB, col_count, NB).transpose(0, 3, 1, 2, 4)
    u_blocks = u_cay.reshape(row_count, NB, NB)
    v_blocks = v_cay.reshape(NB, col_count, NB).transpose(1, 0, 2)
    row_ids = jnp.arange(row_count, dtype=jnp.int32)
    col_ids = jnp.arange(col_count, dtype=jnp.int32)
    first_cols = (FRONT - row_ids).astype(jnp.int32)
    second_cols = (FRONT + 1 - row_ids).astype(jnp.int32)
    first_x = jax.vmap(solve_block)(u_blocks, v_blocks[first_cols], blocks[row_ids, first_cols])
    above = jnp.concatenate([jnp.zeros((1, NB, NB), first_x.dtype), first_x[:-1]], axis=0)
    a_near = a_blocks[row_ids, second_cols, 0]
    b_near = b_blocks[row_ids, second_cols, 0]
    right_side = blocks[row_ids, second_cols] - (jax.vmap(product)(a_near, above) + jax.vmap(product)(first_x, b_near))
    second_x = jax.vmap(solve_block)(u_blocks, v_blocks[second_cols], right_side)
    first_rows = (FRONT - col_ids).astype(jnp.int32)
    second_rows = (FRONT + 1 - col_ids).astype(jnp.int32)
    first_valid = (first_rows >= 0) & (first_rows < row_count)
    second_valid = (second_rows >= 0) & (second_rows < row_count)
    col_first = jnp.where(first_valid[:, None, None], first_x[jnp.clip(first_rows, 0, row_count - 1)], 0.0)
    col_second = jnp.where(second_valid[:, None, None], second_x[jnp.clip(second_rows, 0, row_count - 1)], 0.0)
    col_stack = jnp.stack([col_first, col_second])
    row_stack = jnp.stack([first_x, second_x])
    a_term = jnp.einsum('ijfab,fjbc->ijac', a_blocks, col_stack, precision=precise)
    b_term = jnp.einsum('fiab,ijfbc->ijac', row_stack, b_blocks, precision=precise)
    updated = blocks - (a_term + b_term)
    block_sum = row_ids[:, None] + col_ids[None, :]
    result = jnp.where((block_sum >= FRONT + 2)[:, :, None, None], updated, blocks)
    result = result.at[row_ids, first_cols].set(first_x)
    result = result.at[row_ids, second_cols].set(second_x)
    return result.transpose(0, 2, 1, 3).reshape(N, M)
```

```python
import functools

import jax
import jax.numpy as jnp
from jax import lax
from jax.experimental import pallas as pl
from jax.experimental.pallas import tpu as pltpu
from jax.sharding import PartitionSpec as P


ITERS = 3
SIDE = 4
ROW_TREE = (
    (((0, 5),), ((0, -5),)),
    (((0, 1), (5, 7), (-5, -4)), ((0, -1), (5, 4), (-5, -6))),
    (((1, 2), (7, 8), (-4, -3)), ((-1, -2), (4, 3), (7, 6), (-6, -7))),
)
COL_TREE = (
    ((((0, 0), (1, 2)),), (((0, 0), (2, 3)),), (((0, 0), (3, 1)),)),
    (
        (((0, 0), (0, 3)), ((1, 2), (0, 2)), ((2, 3), (1, 3)), ((3, 1), (3, 0))),
        (((0, 0), (0, 1)), ((1, 2), (2, 2)), ((2, 3), (3, 3)), ((3, 1), (3, 2))),
        (((0, 0), (1, 0)), ((1, 2), (1, 1)), ((2, 3), (2, 0)), ((3, 1), (2, 1))),
    ),
)


def prune(edges, wanted):
    parent = {target: source for _, _, source, target in edges}
    alive = set()
    for node in wanted:
        while node in parent and node not in alive:
            alive.add(node)
            node = parent[node]
    return [edge for edge in edges if edge[3] in alive]


def row_plan(rows, cols, front):
    rounds = [[[] for _ in ops] for ops in ROW_TREE]
    swap = []
    chips = cols // 2
    for i in range(rows):
        source = front - i
        zed, core = divmod(source, 2)
        wanted = [j for j in range(cols) if i + j > rows]
        edges = []
        for k, ops in enumerate(ROW_TREE):
            for n, op in enumerate(ops):
                for a, b in op:
                    edges.append((k, n, (zed + a) % chips, (zed + b) % chips))
        kept = prune(edges, {j // 2 for j in wanted})
        for k, n, a, b in kept:
            rounds[k][n].append((i * cols + 2 * a + core, i * cols + 2 * b + core))
        for j in wanted:
            if j % 2 != core:
                swap.append((i * cols + (j ^ 1), i * cols + j))
    return rounds, swap


def col_plan(rows, cols, front):
    rounds = [[[] for _ in ops] for ops in COL_TREE]
    for j in range(cols):
        source = front - j
        if not 0 <= source < rows:
            continue
        sx, sy = divmod(source, SIDE)

        def place(node):
            dx, dy = node if j % 2 == 0 else (node[1], node[0])
            return (sx + dx) % SIDE * SIDE + (sy + dy) % SIDE

        edges = []
        for k, ops in enumerate(COL_TREE):
            for n, op in enumerate(ops):
                for a, b in op:
                    edges.append((k, n, place(a), place(b)))
        kept = prune(edges, {i for i in range(rows) if i + j > rows})
        for k, n, a, b in kept:
            rounds[k][n].append((a * cols + j, b * cols + j))
    return rounds


def send(value, pairs):
    return lax.ppermute(value, ("row", "col"), pairs)


def total(*values):
    return functools.reduce(jnp.add, values)


def parts(x):
    high = x.astype(jnp.bfloat16)
    return high, (x - high.astype(jnp.float32)).astype(jnp.bfloat16)


def left(x):
    high, low = parts(x)
    return jnp.concatenate([high, high, low], axis=1)


def right(x):
    high, low = parts(x)
    return jnp.concatenate([high, low, high], axis=0)


def times(a, b):
    return jnp.dot(a, b, preferred_element_type=jnp.float32)


def place_of():
    return lax.axis_index("row") + lax.axis_index("col")


def fetch(pairs, sems):
    copies = [pltpu.make_async_copy(src, dst, sems.at[n]) for n, (src, dst) in enumerate(pairs)]
    for copy in copies:
        copy.start()
    for copy in copies:
        copy.wait()


def first_kernel(front, u_hbm, v_hbm, r_hbm, x_ref, up_ref, vp_ref, u_ref, v_ref, r_ref, sems):
    place = place_of()

    @pl.when(place == front)
    def _():
        fetch([(u_hbm, u_ref), (v_hbm, v_ref), (r_hbm, r_ref)], sems)
        u, v, r = u_ref[...], v_ref[...], r_ref[...]
        p = r + times(left(u), right(r))
        w = 0.5 * (p + times(left(p), right(v)))
        for k in range(ITERS):
            w = w + times(left(u), right(times(left(w), right(v))))
            if k + 1 < ITERS:
                u = times(left(u), right(u))
                v = times(left(v), right(v))
        x_ref[...] = w

    @pl.when(place != front)
    def _():
        x_ref[...] = jnp.zeros_like(x_ref)

    @pl.when(place == front + 1)
    def _():
        fetch([(u_hbm, u_ref), (v_hbm, v_ref)], sems)
        u, v = u_ref[...], v_ref[...]
        for k in range(ITERS):
            up_ref[k] = left(u)
            vp_ref[k] = right(v)
            if k + 1 < ITERS:
                u = times(up_ref[k], right(u))
                v = times(left(v), vp_ref[k])


def second_kernel(front, a_hbm, b_hbm, r_hbm, xu_hbm, xl_hbm, up_hbm, vp_hbm, x_ref,
                  a_ref, b_ref, r_ref, xu_ref, xl_ref, up_ref, vp_ref, sems):
    place = place_of()
    n = r_ref.shape[0]

    @pl.when(place == front + 1)
    def _():
        fetch([(a_hbm.at[:, pl.ds(0, n)], a_ref), (b_hbm.at[pl.ds(0, n)], b_ref), (r_hbm, r_ref),
               (xu_hbm, xu_ref), (xl_hbm, xl_ref), (up_hbm, up_ref), (vp_hbm, vp_ref)], sems)
        r = r_ref[...] - (times(left(a_ref[...]), right(xu_ref[...])) + times(left(xl_ref[...]), right(b_ref[...])))
        p = r + times(up_ref[0], right(r))
        w = 0.5 * (p + times(left(p), vp_ref[0]))
        for k in range(ITERS):
            w = w + times(up_ref[k], right(times(left(w), vp_ref[k])))
        x_ref[...] = w

    @pl.when(place != front + 1)
    def _():
        x_ref[...] = jnp.zeros_like(x_ref)


def near_kernel(front, a_hbm, b_hbm, r_hbm, c_hbm, x_hbm, o_ref, a_ref, b_ref, r_ref, c_ref, x_ref, sems):
    place = place_of()
    n = r_ref.shape[0]

    @pl.when(place > front + 1)
    def _():
        fetch([(a_hbm.at[:, pl.ds(0, n)], a_ref), (b_hbm.at[pl.ds(0, n)], b_ref), (r_hbm, r_ref),
               (c_hbm, c_ref), (x_hbm, x_ref)], sems)
        o_ref[...] = r_ref[...] - (
            times(left(a_ref[...]), right(c_ref[...])) + times(left(x_ref[...]), right(b_ref[...])))


def last_kernel(front, a_hbm, b_hbm, r_hbm, t_hbm, c_hbm, x_hbm, f_hbm, s_hbm, o_hbm,
                a_ref, b_ref, t_ref, c_ref, x_ref, o_ref, sems):
    place = place_of()
    n = t_ref.shape[0]

    @pl.when(place > front + 1)
    def _():
        fetch([(a_hbm.at[:, pl.ds(n, n)], a_ref), (b_hbm.at[pl.ds(n, n)], b_ref), (t_hbm, t_ref),
               (c_hbm, c_ref), (x_hbm, x_ref)], sems)
        o_ref[...] = t_ref[...] - (
            times(left(a_ref[...]), right(c_ref[...])) + times(left(x_ref[...]), right(b_ref[...])))
        fetch([(o_ref, o_hbm)], sems)

    @pl.when(place == front + 1)
    def _():
        fetch([(s_hbm, o_hbm)], sems)

    @pl.when(place == front)
    def _():
        fetch([(f_hbm, o_hbm)], sems)

    @pl.when(place < front)
    def _():
        fetch([(r_hbm, o_hbm)], sems)


def call(kernel, front, args, outs, scratch, name, out_spec=None):
    count = len(args)
    any_space = pl.BlockSpec(memory_space=pl.ANY)
    vmem = pl.BlockSpec(memory_space=pltpu.VMEM)
    return pl.pallas_call(
        functools.partial(kernel, front),
        out_shape=outs,
        in_specs=[any_space] * count,
        out_specs=jax.tree.map(lambda _: out_spec or vmem, outs),
        scratch_shapes=[pltpu.VMEM(shape, dtype) for shape, dtype in scratch] + [pltpu.SemaphoreType.DMA((8,))],
        name=name,
    )(*args)


def body(rows, cols, rhs, a_pair, b_pair, u_cay, v_cay):
    front = rows - 1
    n = rhs.shape[0]
    block = jax.ShapeDtypeStruct((n, n), jnp.float32)
    one = ((n, n), jnp.float32)
    ups = jax.ShapeDtypeStruct((ITERS, n, 3 * n), jnp.bfloat16)
    vps = jax.ShapeDtypeStruct((ITERS, 3 * n, n), jnp.bfloat16)

    first, ups_v, vps_v = call(first_kernel, front, (u_cay, v_cay, rhs), (block, ups, vps), [one] * 3, "first")

    hop_down = [((i - 1) * cols + rows - i, i * cols + rows - i) for i in range(1, rows)]
    hop_over = [(i * cols + front - i, i * cols + rows - i) for i in range(rows)]
    down = send(first, hop_down)
    over = send(first, hop_over)

    def row_start(x, plan):
        return [send(x, op) for op in plan[0][0]]

    def row_finish(x, got, plan):
        rounds, swap = plan
        have = total(x, *got)
        second = [send(have, op) for op in rounds[1]]
        have2 = total(*second)
        third = [send(second[0], rounds[2][0]), send(have2, rounds[2][1])]
        whole = total(have, have2, *third)
        return whole + send(whole, swap)

    def col_start(x, plan):
        return [send(x, op) for op in plan[0]]

    def col_finish(x, got, plan):
        have = total(x, *got)
        return total(*got, *[send(have, op) for op in plan[1]])

    row_one, col_one = row_plan(rows, cols, front), col_plan(rows, cols, front)
    row_two, col_two = row_plan(rows, cols, front + 1), col_plan(rows, cols, front + 1)

    rg, cg = row_start(first, row_one), col_start(first, col_one)
    second = call(second_kernel, front, (a_pair, b_pair, rhs, down, over, ups_v, vps_v), block,
                  [one] * 5 + [(ups.shape, ups.dtype), (vps.shape, vps.dtype)], "second")
    row_first, col_first = row_finish(first, rg, row_one), col_finish(first, cg, col_one)
    near = call(near_kernel, front, (a_pair, b_pair, rhs, col_first, row_first), block, [one] * 5, "near")
    rg2, cg2 = row_start(second, row_two), col_start(second, col_two)
    row_second, col_second = row_finish(second, rg2, row_two), col_finish(second, cg2, col_two)
    return call(last_kernel, front, (a_pair, b_pair, rhs, near, col_second, row_second, first, second), block,
                [one] * 6, "last", pl.BlockSpec(memory_space=pl.ANY))


def solution(mesh):
    rows, cols = mesh.shape["row"], mesh.shape["col"]
    placed = (P("row", "col"), P("row", "col"), P("row", "col"), P("row", None), P(None, "col"))
    return jax.shard_map(
        functools.partial(body, rows, cols), mesh=mesh, in_specs=placed, out_specs=P("row", "col"), check_vma=False
    )
```
